32 devices in a mesh: cp: 2 (over x), fsdp: 16 (over z, y, core).
Axes of the slice: x: 2, y: 2, z: 4, core: 2. Of those that a mesh axis runs over, the one named last changes fastest.
Arguments:
- hidden: bfloat16 [16, 256, 16384], P('fsdp', 'cp'), may hold values from -6 to 6
- norm_gain: bfloat16 [16384], P('fsdp'), may hold values from 0.25 to 1.75
- query_weight: bfloat16 [16384, 256], P('fsdp'), may hold values from -0.0625 to 0.0625
- key_weight: bfloat16 [16384, 128], P('fsdp'), may hold values from -0.0625 to 0.0625
- value_weight: bfloat16 [16384, 128], P('fsdp'), may hold values from -0.046875 to 0.046875
- out_weight: bfloat16 [256, 16384], P(None, 'fsdp'), may hold values from -0.75 to 0.75
- doc_lengths: int32 [16, 4], P('fsdp'), may hold values from 1 to 128, 256 in all within a row
Outputs:
- attention_out: bfloat16 [16, 256, 16384], P('fsdp', 'cp')
The draws below stay inside these ranges and needn't reach their ends.
Inputs may be any that keep to these rules, and one draw needn't show every extreme that they name: `doc_lengths`: each row holds the lengths of the 4 documents of one sequence in order; they sum to 256 and the longest is exactly 128.
All inputs are finite; a program needn't handle non-finite values.
Results may differ from the reference program's by a relative error of at most 0.012.
Values may be sent and summed in bfloat16 or wider, within the bound.
No kernel may reach another device: no remote copies, remote signals or barrier semaphores. Data moves between devices by JAX's collectives and lax.ppermute only.
A program may use at most 128 MiB of HBM per device.

```python
import math
import jax
import jax.numpy as jnp
import numpy as np
from jax import lax

D = 16384
HD = 128
QH = 2
NDOC = 4
SEQS = 16
SEQLEN = 256
MOSTDOC = 128


def steps_of(key, extent, pieces, least, largest):
    gain, own = 1.0, jax.random.fold_in(key, 6)
    for dim, blocks in pieces:
        steps = jnp.exp(jax.random.uniform(jax.random.fold_in(own, dim), (blocks,), jnp.float32, least / len(pieces), largest / len(pieces)))
        gain = gain * jnp.repeat(steps, extent[dim] // blocks).reshape([-1 if axis == dim else 1 for axis in range(len(extent))])
    return gain


def split_up(amount, total, limit, slope):
    weights = [(1 << 20) // math.isqrt(standing ** slope) + 1 for standing in range(2, amount + 1)]
    rest, holding = total - limit - (amount - 1), [1] * (amount - 1)
    while rest > 0:
        candidates = [i for i in range(amount - 1) if holding[i] < limit]
        whole, budget = sum([weights[i] for i in candidates]), rest
        for i in candidates:
            more = min(limit - holding[i], max(1, budget * weights[i] // whole), rest)
            holding[i] = holding[i] + more
            rest = rest - more
    return np.array([limit] + holding)


def uneven_parts(rng, amount, total, bound, lean):
    if amount == 2:
        one = jax.random.randint(rng, (), max(1, total - bound), min(bound, total - 1) + 1)
        return jnp.stack([one, total - one])
    sizes = jnp.asarray(split_up(amount, total, bound, lean), jnp.int32)
    pairs = (amount - 1) // 2
    source_of, taker = sizes[1:1 + 2 * pairs:2], sizes[2:2 + 2 * pairs:2]
    room = jnp.minimum(source_of - 1, bound - taker)
    shifted = jax.random.randint(jax.random.fold_in(rng, 1), (pairs,), 0, 1 << 20) % (room + 1)
    sizes = sizes.at[1:1 + 2 * pairs:2].set(source_of - shifted).at[2:2 + 2 * pairs:2].set(taker + shifted)
    return sizes[jax.random.permutation(jax.random.fold_in(rng, 2), amount)]


def noise(own_key, dims, width, most, pieces=(), held_as=jnp.bfloat16):
    factor_of = steps_of(own_key, dims, pieces, -0.22, 0.18) if pieces else 1.0
    array = jax.random.normal(own_key, dims, jnp.float32) * width * factor_of
    return jnp.minimum(jnp.maximum(array, -most), most).astype(held_as)


def setup_inputs(seed: int = 0) -> dict:
    streams_of = jax.random.split(jax.random.key(seed), 8)
    hidden = noise(streams_of[0], (SEQS, SEQLEN, D), 1.0, 6.0, ((0, 16), (1, 2)))
    norm_gain = jnp.clip(1.0 + 0.15 * jax.random.normal(streams_of[1], (D,), jnp.float32), 0.25, 1.75).astype(jnp.bfloat16)
    query_weight = noise(streams_of[2], (D, QH * HD), (D // 2) ** -0.5, 0.0625, ((0, 16),))
    key_weight = noise(streams_of[3], (D, HD), (D // 2) ** -0.5, 0.0625, ((0, 16),))
    value_weight = noise(streams_of[4], (D, HD), D ** -0.5, 0.046875, ((0, 16),))
    out_weight = noise(streams_of[5], (QH * HD, D), (QH * HD // 4) ** -0.5, 0.75, ((1, 16),))
    doc_lengths = jax.vmap(lambda own: uneven_parts(own, NDOC, SEQLEN, MOSTDOC, 2))(jax.random.split(streams_of[6], SEQS)).reshape((SEQS, NDOC)).astype(jnp.int32)
    return dict(hidden=hidden, norm_gain=norm_gain, query_weight=query_weight, key_weight=key_weight, value_weight=value_weight, out_weight=out_weight, doc_lengths=doc_lengths)


EPSILON = 1e-05
THETA = 500000.0

def rounded(values):
    return lax.optimization_barrier(values.astype(jnp.bfloat16))

def doc_tables(lengths, total):
    lengths = lengths.astype(jnp.int32)
    ends = jnp.cumsum(lengths).astype(jnp.int32)
    starts = (ends - lengths).astype(jnp.int32)
    places = jnp.arange(total, dtype=jnp.int32)
    after = (ends[None, :] <= places[:, None]).astype(jnp.int32)
    doc_ids = lax.optimization_barrier(jnp.sum(after, axis=1)).astype(jnp.int32)
    member = (doc_ids[:, None] == jnp.arange(lengths.shape[0], dtype=jnp.int32)[None, :]).astype(jnp.int32)
    offsets = (places - lax.optimization_barrier(jnp.sum(member * starts[None, :], axis=1))).astype(jnp.int32)
    return (doc_ids, offsets)

def rotate(values, offsets):
    head_dim = values.shape[2]
    half = head_dim // 2
    rates = jnp.power(THETA, -2.0 * jnp.arange(half, dtype=jnp.float32) / head_dim)
    angles = offsets.astype(jnp.float32)[:, None] * rates[None, :]
    cosine = jnp.cos(angles)[:, None, :]
    sine = jnp.sin(angles)[:, None, :]
    first = values[:, :, :half]
    second = values[:, :, half:]
    return jnp.concatenate([first * cosine - second * sine, second * cosine + first * sine], axis=2)

def one_sequence(hidden, lengths, norm_gain, query_weight, key_weight, value_weight, out_weight):
    total = hidden.shape[0]
    head_dim = key_weight.shape[1]
    heads = query_weight.shape[1] // head_dim
    doc_ids, offsets = doc_tables(lengths, total)
    tokens = hidden.astype(jnp.float32)
    scaled = tokens * lax.rsqrt(lax.optimization_barrier(jnp.mean(tokens * tokens, axis=1, keepdims=True)) + EPSILON)
    normed = (scaled * norm_gain.astype(jnp.float32)[None, :]).astype(jnp.bfloat16)
    query_raw = jnp.dot(normed, query_weight, preferred_element_type=jnp.float32)
    key_raw = jnp.dot(normed, key_weight, preferred_element_type=jnp.float32)
    value = rounded(jnp.dot(normed, value_weight, preferred_element_type=jnp.float32))
    query = rounded(rotate(query_raw.reshape(total, heads, head_dim), offsets) * head_dim ** (-0.5))
    key = rounded(rotate(key_raw.reshape(total, 1, head_dim), offsets)[:, 0, :])
    scores = jnp.einsum('qhd,kd->hqk', query.astype(jnp.float32), key.astype(jnp.float32))
    places = jnp.arange(total, dtype=jnp.int32)
    allowed = jnp.logical_and(doc_ids[:, None] == doc_ids[None, :], places[None, :] <= places[:, None])
    weights = jnp.where(allowed[None, :, :], jnp.exp(scores), jnp.float32(0.0))
    totals = lax.optimization_barrier(jnp.sum(weights, axis=2))
    weights_rounded = rounded(weights)
    summed = jnp.einsum('hqk,kd->hqd', weights_rounded.astype(jnp.float32), value.astype(jnp.float32))
    attended = (summed / totals[:, :, None]).astype(jnp.bfloat16)
    attended = attended.transpose(1, 0, 2).reshape(total, heads * head_dim)
    return jnp.dot(attended, out_weight, preferred_element_type=jnp.float32).astype(jnp.bfloat16)

def reference(hidden, norm_gain, query_weight, key_weight, value_weight, out_weight, doc_lengths):

    def per_sequence(pair):
        return one_sequence(pair[0], pair[1], norm_gain, query_weight, key_weight, value_weight, out_weight)
    return lax.map(per_sequence, (hidden, doc_lengths))
```

```python
import functools

import jax
import jax.numpy as jnp
from jax import lax
from jax.experimental import pallas as pl
from jax.experimental.pallas import tpu as pltpu
from jax.sharding import PartitionSpec as P

EPSILON = 1e-05
THETA = 500000.0
GROUP = 4


WHOLE = pl.BlockSpec(memory_space=pltpu.VMEM)
SCALARS = pl.BlockSpec(memory_space=pltpu.SMEM)


def offsets_of(lengths, places):
    ends = jnp.cumsum(lengths)
    inside = (ends[None, :] <= places[:, None]).astype(jnp.int32)
    return places - jnp.sum(inside * lengths[None, :], axis=1)


def rope_tables(offsets, head_dim):
    half = head_dim // 2
    rates = jnp.power(THETA, -2.0 * jnp.arange(half, dtype=jnp.float32) / head_dim)
    angles = offsets.astype(jnp.float32)[:, None] * rates[None, :]
    cosine, sine = jnp.cos(angles), jnp.sin(angles)
    return (
        jnp.concatenate([cosine, cosine], axis=1),
        jnp.concatenate([-sine, sine], axis=1),
    )


def first_round(rows, place, h0, h1, h2, h3, weight, acc):
    tokens = jnp.concatenate([h0[...], h1[...], h2[...], h3[...]], axis=0)
    acc[...] = jnp.dot(tokens, weight[...], preferred_element_type=jnp.float32)


def add_round(place, h0, h1, h2, h3, own_a, own_b, other_a, other_b, before, *outs):
    quarter = own_a.shape[0]
    side = place[1]
    total = before[...]
    for base, piece in (
        (side * 2, own_a),
        (side * 2 + 1, own_b),
        ((1 - side) * 2, other_a),
        ((1 - side) * 2 + 1, other_b),
    ):
        columns = pl.ds(pl.multiple_of(base * quarter, quarter), quarter)
        tokens = jnp.concatenate([h[:, columns] for h in (h0, h1, h2, h3)], axis=0)
        total = total + jnp.dot(tokens, piece[...], preferred_element_type=jnp.float32)
    if len(outs) == 1:
        outs[0][...] = total
    else:
        rows = h0.shape[0]
        for member, out in enumerate(outs):
            out[...] = total[member * rows : (member + 1) * rows].astype(out.dtype)


def merge_parts(head_dim, own, p1, p2, p3, scale, cosine, sine, q_out, kv_out):
    raw = own[...] + p1[...].astype(jnp.float32)
    raw = raw + (p2[...].astype(jnp.float32) + p3[...].astype(jnp.float32))
    raw = raw * scale[...]
    cos, sin = cosine[...], sine[...]

    def rot(u):
        return u * cos + pltpu.roll(u, head_dim // 2, 1) * sin

    wide = q_out.shape[1]
    for head in range(wide // head_dim):
        part = slice(head * head_dim, (head + 1) * head_dim)
        q_out[:, part] = (rot(raw[:, part]) * head_dim**-0.5).astype(q_out.dtype)
    kv_out[:, :head_dim] = rot(raw[:, wide : wide + head_dim]).astype(kv_out.dtype)
    kv_out[:, head_dim:] = raw[:, wide + head_dim :].astype(kv_out.dtype)


def attend(head_dim, groups, docs, info, q_ref, *refs):
    kvs, out = refs[:-1], refs[-1]
    rows = q_ref.shape[0]
    here = info[0]
    ends, run = [], jnp.int32(0)
    for j in range(docs):
        run = run + info[1 + j]
        ends.append(run)

    def doc_of(places):
        found = jnp.zeros(places.shape, jnp.int32)
        for end in ends:
            found = found + (end <= places).astype(jnp.int32)
        return found

    shape = (rows, rows)
    q_places = here * rows + lax.broadcasted_iota(jnp.int32, shape, 0)
    q_docs = doc_of(q_places)
    masks = []
    for k in range(groups):
        there = lax.rem(here + groups - k, groups)
        k_places = there * rows + lax.broadcasted_iota(jnp.int32, shape, 1)
        masks.append(jnp.logical_and(doc_of(k_places) == q_docs, k_places <= q_places))
    for head in range(q_ref.shape[1] // head_dim):
        part = slice(head * head_dim, (head + 1) * head_dim)
        query = q_ref[:, part]
        denom = jnp.zeros((rows, 1), jnp.float32)
        numer = jnp.zeros((rows, head_dim), jnp.float32)
        for kv, mask in zip(kvs, masks):
            scores = lax.dot_general(
                query, kv[:, :head_dim], (((1,), (1,)), ((), ())), preferred_element_type=jnp.float32
            )
            e = jnp.where(mask, jnp.exp(scores), jnp.float32(0.0))
            denom = denom + jnp.sum(e, axis=1, keepdims=True)
            numer = numer + jnp.dot(
                e.astype(jnp.bfloat16), kv[:, head_dim:], preferred_element_type=jnp.float32
            )
        out[:, part] = (numer / denom).astype(out.dtype)


def project(count, aliased, place, att, *refs):
    pieces, out = refs[: 2 * count], refs[-1]
    step = pl.program_id(0)
    half = att.shape[1] // 2
    side = place[count]
    for k in range(count):

        @pl.when(step == k)
        def _():
            own, other = pieces[2 * k], pieces[2 * k + 1]
            mine = att[:, pl.ds(pl.multiple_of(side * half, half), half)]
            theirs = att[:, pl.ds(pl.multiple_of((1 - side) * half, half), half)]
            total = jnp.dot(mine, own[...], preferred_element_type=jnp.float32)
            total = total + jnp.dot(theirs, other[...], preferred_element_type=jnp.float32)
            out[...] = total.astype(out.dtype)


def local(hidden, norm_gain, query_weight, key_weight, value_weight, out_weight, doc_lengths):
    tokens = hidden[0]
    rows, width = tokens.shape
    head_dim = key_weight.shape[1]
    docs = doc_lengths.shape[1]
    groups, shards = lax.axis_size("cp"), lax.axis_size("fsdp")
    here, me = lax.axis_index("cp"), lax.axis_index("fsdp")
    span = query_weight.shape[0]
    line = shards // GROUP
    spot, member = me // GROUP, me % GROUP
    side = here % 2

    def swap(a, bits):
        return lax.ppermute(a, "fsdp", [(i, i ^ bits) for i in range(shards)])

    def across(a):
        return lax.ppermute(a, "cp", [(i, i ^ 1) for i in range(groups)])

    def shift(a, by):
        pairs = [(i, (i // GROUP + by) % line * GROUP + i % GROUP) for i in range(shards)]
        return lax.ppermute(a, "fsdp", pairs)

    order = [0, 1, line - 1, 2] if line == 4 else list(range(line))

    joined = jnp.concatenate([query_weight, key_weight, value_weight], axis=1)
    joined = (joined.astype(jnp.float32) * norm_gain.astype(jnp.float32)[:, None]).astype(jnp.bfloat16)
    quarter = span // 4
    own_a = lax.dynamic_slice_in_dim(joined, side * 2 * quarter, quarter, 0)
    own_b = lax.dynamic_slice_in_dim(joined, (side * 2 + 1) * quarter, quarter, 0)

    def chunk(back, q):
        index = (spot + line - back) % line * GROUP + (member ^ q)
        return lax.dynamic_slice_in_dim(tokens, index * span, span, 1)

    sent = {}
    for back in order:
        for q in (2, 3, 1):
            sent[back, q] = swap(chunk(back, q), q)

    arrived = {}
    if line == 4:
        p1a, m1a = shift(own_a, 1), shift(own_a, -1)
        p1b, m1b = shift(own_b, 1), shift(own_b, -1)
        p2a, m2b = shift(p1a, 1), shift(m1b, -1)
        arrived = {1: (p1a, p1b), 3: (m1a, m1b), 2: (p2a, m2b)}
    else:
        for back in order[1:]:
            arrived[back] = (shift(own_a, back), shift(own_b, back))
    others = {back: tuple(across(a) for a in arrived[back]) for back in order[1:]}

    wide = tokens.astype(jnp.float32)
    scale = lax.rsqrt(jnp.mean(wide * wide, axis=1, keepdims=True) + EPSILON)
    places = here * rows + jnp.arange(rows, dtype=jnp.int32)
    cosine, sine = rope_tables(offsets_of(doc_lengths[0], places), head_dim)

    features = joined.shape[1]
    total = None
    own_spec = pl.BlockSpec((rows, span), lambda i, place: (0, place[0]))
    for back in order:
        place = jnp.stack([(spot + line - back) % line * GROUP + member, side]).astype(jnp.int32)
        last = back == order[-1]
        if last:
            kinds = [jnp.float32] + [jnp.bfloat16] * (GROUP - 1)
            out_shape = [jax.ShapeDtypeStruct((rows, features), kind) for kind in kinds]
        else:
            out_shape = jax.ShapeDtypeStruct((GROUP * rows, features), jnp.float32)
        if total is None:
            body, operands = functools.partial(first_round, rows), [joined]
        else:
            body = add_round
            operands = [*arrived[back], *others[back], total]
        hs = [sent[back, q] for q in (1, 2, 3)]
        total = pl.pallas_call(
            body,
            out_shape=out_shape,
            grid_spec=pltpu.PrefetchScalarGridSpec(
                num_scalar_prefetch=1,
                grid=(1,),
                in_specs=[own_spec] + [WHOLE] * (len(hs) + len(operands)),
                out_specs=[WHOLE] * GROUP if last else WHOLE,
            ),
            cost_estimate=pl.CostEstimate(
                flops=2 * GROUP * rows * span * features,
                bytes_accessed=2 * GROUP * rows * span + 8 * GROUP * rows * features,
                transcendentals=0,
            ),
            name=f"partial_{back}",
        )(place, tokens, *hs, *operands)
    parts = [total[0]] + [swap(total[q], q) for q in (1, 2, 3)]

    q_rows, kv_rows = pl.pallas_call(
        functools.partial(merge_parts, head_dim),
        out_shape=[
            jax.ShapeDtypeStruct((rows, query_weight.shape[1]), jnp.bfloat16),
            jax.ShapeDtypeStruct((rows, 2 * head_dim), jnp.bfloat16),
        ],
        in_specs=[WHOLE] * 7,
        out_specs=[WHOLE] * 2,
        name="merge_parts",
    )(*parts, scale, cosine, sine)

    kvs = [kv_rows]
    for k in range(1, groups):
        kvs.append(lax.ppermute(kv_rows, "cp", [(i, (i + k) % groups) for i in range(groups)]))
    info = jnp.concatenate([here[None].astype(jnp.int32), doc_lengths[0]])
    attended = pl.pallas_call(
        functools.partial(attend, head_dim, groups, docs),
        out_shape=jax.ShapeDtypeStruct(q_rows.shape, jnp.bfloat16),
        in_specs=[SCALARS] + [WHOLE] * (1 + groups),
        out_specs=WHOLE,
        name="attend",
    )(info, q_rows, *kvs)

    half = out_weight.shape[0] // 2
    mine = lax.dynamic_slice_in_dim(out_weight, side * half, half, 0)
    theirs = lax.dynamic_slice_in_dim(out_weight, (1 - side) * half, half, 0)
    near = {(0, 0): mine}
    for back in order[1:]:
        near[back, 0] = shift(mine, -1 if back == line - 1 else back)
    for back in order:
        near[back, 2] = swap(near[back, 0], 2)
    full = {}
    for back in order:
        for flip in (0, 2):
            far = theirs if (back, flip) == (0, 0) else across(near[back, flip])
            full[back, flip] = (near[back, flip], far)
    for back in order:
        for flip in (0, 2):
            full[back, flip + 1] = tuple(swap(a, 1) for a in full[back, flip])

    result = None
    cut = max(1, line - 1)
    for batch in (order[:cut], order[cut:]):
        keys = [(back, flip) for back in batch for flip in range(GROUP)]
        if not keys:
            continue
        place = jnp.stack(
            [(spot + line - back) % line * GROUP + (member ^ flip) for back, flip in keys] + [side]
        ).astype(jnp.int32)
        pieces = [a for key in keys for a in full[key]]
        extra = [] if result is None else [result]
        result = pl.pallas_call(
            functools.partial(project, len(keys), bool(extra)),
            out_shape=jax.ShapeDtypeStruct((rows, width), jnp.bfloat16),
            grid_spec=pltpu.PrefetchScalarGridSpec(
                num_scalar_prefetch=1,
                grid=(len(keys),),
                in_specs=[WHOLE] * (1 + len(pieces)) + [pl.BlockSpec(memory_space=pl.ANY)] * len(extra),
                out_specs=pl.BlockSpec((rows, span), lambda i, place: (0, place[i])),
            ),
            input_output_aliases={2 + len(pieces): 0} if extra else {},
            name=f"project_{len(keys)}",
        )(place, attended, *pieces, *extra)
    return result[None, :, :]


def solution(mesh):
    in_specs = (
        P("fsdp", "cp", None),
        P("fsdp"),
        P("fsdp", None),
        P("fsdp", None),
        P("fsdp", None),
        P(None, "fsdp"),
        P("fsdp", None),
    )
    out_specs = P("fsdp", "cp", None)
    return jax.shard_map(local, mesh=mesh, in_specs=in_specs, out_specs=out_specs, check_vma=False)
```
